32 devices in a mesh: ctx: 8 (over y, x, core), tp: 4 (over z).
Axes of the slice: x: 2, y: 2, z: 4, core: 2. Of those that a mesh axis runs over, the one named last changes fastest.
Arguments:
- query_rows: bfloat16 [8192, 4096], P('ctx', 'tp'), may hold values from -6 to 6
- key_rows: bfloat16 [8192, 4096], P('ctx', 'tp'), may hold values from -6 to 6
- value_rows: bfloat16 [8192, 4096], P('ctx', 'tp'), may hold values from -6 to 6
- layer_grad: bfloat16 [8192, 4096], P('ctx', 'tp'), may hold values from -6 to 6
- out_weight: bfloat16 [4096, 4096], P('tp'), may hold values from -0.09375 to 0.09375
Outputs:
- query_grad: bfloat16 [8192, 4096], P('ctx', 'tp')
- key_grad: bfloat16 [8192, 4096], P('ctx', 'tp')
- value_grad: bfloat16 [8192, 4096], P('ctx', 'tp')
The draws below stay inside these ranges and needn't reach their ends.
All inputs are finite; a program needn't handle non-finite values.
Results may differ from the reference program's by a relative error of at most 0.0058.
Values may be sent and summed in bfloat16 or wider, within the bound.
A program may use at most 128 MiB of HBM per device.

```python
import jax
import jax.numpy as jnp
from jax import lax

D = 4096
HEADS = 32
HEAD = 128
TOK_DEV = 1024
TOKENS = 8192
N_CTX = 8


def level_of(key, extent, split, smallest, top_value):
    def one(dim, blocks):
        heights = jax.random.uniform(jax.random.fold_in(jax.random.fold_in(key, 6), dim), (blocks,), jnp.float32, smallest / len(split), top_value / len(split))
        return jnp.repeat(jnp.exp(heights), extent[dim] // blocks).reshape((-1,) + (1,) * (len(extent) - dim - 1))

    gain = one(*split[0])
    for cut in split[1:]:
        gain = gain * one(*cut)
    return gain


def noise(stream_key, shape, spread, most, cuts=(), kind=jnp.bfloat16):
    gain = level_of(stream_key, shape, cuts, -0.22, 0.18) if cuts else 1.0
    result = jax.random.normal(stream_key, shape, jnp.float32) * spread * gain
    return jnp.minimum(jnp.maximum(result, -most), most).astype(kind)


def setup_inputs(seed: int = 0) -> dict:
    splits = jax.random.split(jax.random.key(seed), 6)
    query_rows = noise(splits[0], (TOKENS, HEADS * HEAD), 1.0, 6.0, ((0, 8), (1, 4)))
    key_rows = noise(splits[1], (TOKENS, HEADS * HEAD), 1.0, 6.0, ((0, 8), (1, 4)))
    value_rows = noise(splits[2], (TOKENS, HEADS * HEAD), 1.0, 6.0, ((0, 8), (1, 4)))
    layer_grad = noise(splits[3], (TOKENS, D), 1.0, 6.0, ((0, 8), (1, 4)))
    out_weight = noise(splits[4], (HEADS * HEAD, D), D ** -0.5, 0.09375, ((0, 4),))
    return dict(query_rows=query_rows, key_rows=key_rows, value_rows=value_rows, layer_grad=layer_grad, out_weight=out_weight)


def block_grads(pieces):
    query_blk, key_blk, value_blk, gradient_block, key_value_state, gradient_state = pieces
    factor = (HEAD * TOKENS) ** -0.5
    positions = jnp.arange(TOK_DEV)
    causal = positions[:, None] >= positions[None, :]
    query_float = query_blk.astype(jnp.float32)
    key_float = key_blk.astype(jnp.float32)
    value_float = value_blk.astype(jnp.float32)
    gradient_float = gradient_block.astype(jnp.float32)
    inside_gradient = jnp.einsum("thv,shv->hts", gradient_float, value_float)
    inside_gradient = jnp.where(causal[None], inside_gradient, jnp.float32(0.0)).astype(jnp.bfloat16).astype(jnp.float32)
    inside_query = jnp.einsum("thk,shk->hts", query_float, key_float)
    inside_query = jnp.where(causal[None], inside_query, jnp.float32(0.0)).astype(jnp.bfloat16).astype(jnp.float32)
    key_value_float = key_value_state.astype(jnp.float32)
    gradient_state_float = gradient_state.astype(jnp.float32)
    query_result = jnp.einsum("vmr,rve->mve", inside_gradient, key_float) + jnp.einsum("nde,dze->ndz", gradient_float, key_value_float)
    key_result = jnp.einsum("cxd,xcr->dcr", inside_gradient, query_float) + jnp.einsum("yqr,qmr->yqm", value_float, gradient_state_float)
    value_result = jnp.einsum("kzx,zkm->xkm", inside_query, gradient_float) + jnp.einsum("jaq,aqd->jad", key_float, gradient_state_float)
    return ((factor * query_result).astype(jnp.bfloat16), (factor * key_result).astype(jnp.bfloat16), (factor * value_result).astype(jnp.bfloat16))


def reference(query_rows, key_rows, value_rows, layer_grad, out_weight):
    grad_heads = jnp.dot(layer_grad, out_weight.T, preferred_element_type=jnp.float32).astype(jnp.bfloat16)
    shape4 = (N_CTX, TOK_DEV, HEADS, HEAD)
    query4 = query_rows.reshape(shape4)
    key4 = key_rows.reshape(shape4)
    value4 = value_rows.reshape(shape4)
    grad4 = grad_heads.reshape(shape4)
    key_value_here = jnp.einsum("cthk,cthv->chkv", key4.astype(jnp.float32), value4.astype(jnp.float32))
    gradient_here = jnp.einsum("cthk,cthv->chkv", query4.astype(jnp.float32), grad4.astype(jnp.float32))
    zero_state = jnp.zeros((1, HEADS, HEAD, HEAD), jnp.float32)
    kv_before = jnp.concatenate([zero_state, jnp.cumsum(key_value_here, 0)[:-1]], 0).astype(jnp.bfloat16)
    reversed_sum = jnp.cumsum(gradient_here[::-1], 0)[::-1]
    grad_after = jnp.concatenate([reversed_sum[1:], zero_state], 0).astype(jnp.bfloat16)
    query_result, key_result, value_result = lax.map(block_grads, (query4, key4, value4, grad4, kv_before, grad_after))
    flat = (TOKENS, HEADS * HEAD)
    return (query_result.reshape(flat), key_result.reshape(flat), value_result.reshape(flat))
```

```python
import functools

import jax
import jax.numpy as jnp
from jax import lax
from jax.experimental import pallas as pl
from jax.experimental.pallas import tpu as pltpu
from jax.sharding import PartitionSpec as P

HEAD = 128
MESH = pl.DeviceIdType.MESH
F32 = jnp.float32
BF16 = jnp.bfloat16
NT = (((1,), (1,)), ((), ()))
NN = (((1,), (0,)), ((), ()))
TN = (((0,), (0,)), ((), ()))


def mm(a, b, dims):
    return lax.dot_general(a, b, dims, preferred_element_type=F32)


def attention_head(read, state_kv, state_grad, write, tokens, size, factor):
    count = tokens // size
    pieces = [read(i) for i in range(count)]
    rows = lax.broadcasted_iota(jnp.int32, (size, size), 0)
    cols = lax.broadcasted_iota(jnp.int32, (size, size), 1)
    causal = rows >= cols
    after = [None] * count
    total = state_grad
    for i in reversed(range(count)):
        after[i] = total.astype(BF16)
        if i:
            q, _, _, g = pieces[i]
            total = total + mm(q, g, TN)
    before = state_kv
    for i in range(count):
        q, k, v, g = pieces[i]
        inner_grad = jnp.where(causal, mm(g, v, NT), 0.0).astype(BF16)
        inner_query = jnp.where(causal, mm(q, k, NT), 0.0).astype(BF16)
        query = mm(inner_grad, k, NN) + mm(g, before.astype(BF16), NT)
        key = mm(inner_grad, q, TN) + mm(v, after[i], NT)
        value = mm(inner_query, g, TN) + mm(k, after[i], NN)
        write(i, (factor * query).astype(BF16), (factor * key).astype(BF16), (factor * value).astype(BF16))
        if i < count - 1:
            before = before + mm(k, v, TN)


def attention_kernel(size, factor, q_ref, k_ref, v_ref, g_ref, kv_ref, grad_ref, qo_ref, ko_ref, vo_ref):
    tokens = q_ref.shape[0]

    def read(i):
        at = pl.ds(i * size, size)
        return q_ref[at, :], k_ref[at, :], v_ref[at, :], g_ref[at, :]

    def write(i, query, key, value):
        at = pl.ds(i * size, size)
        qo_ref[at, :] = query
        ko_ref[at, :] = key
        vo_ref[at, :] = value

    attention_head(read, kv_ref[0].astype(F32), grad_ref[0].astype(F32), write, tokens, size, factor)


def attention(q, k, v, g, kv_before, grad_after, factor):
    tokens, columns = q.shape
    size = min(256, tokens)
    rows = pl.BlockSpec((tokens, HEAD), lambda h: (0, h))
    state = pl.BlockSpec((1, HEAD, HEAD), lambda h: (h, 0, 0))
    return pl.pallas_call(
        functools.partial(attention_kernel, size, factor),
        grid=(columns // HEAD,),
        out_shape=[jax.ShapeDtypeStruct(q.shape, BF16)] * 3,
        in_specs=[rows] * 4 + [state] * 2,
        out_specs=[rows] * 3,
    )(q, k, v, g, kv_before, grad_after)


def gather_kernel(
    n_ctx, spans, q_hbm, k_hbm, v_hbm, lg_hbm, w_hbm, qo_buf, key_part, value_part, grad_after, k_buf, v_buf,
    q_buf, g_ref, lg, w, far, part_out, part_in,
    kv_sums, kv_state, state, after,
    kv_out, kv_in, grad_out, grad_twin, pair, pair_in, rest, rest_in,
    load_sem, ends_sem, mids_sem, lg_recv, fwd_sem, end2_recv, part_sem, part_recv,
    far_sem, far_recv, twin_sem, twin_recv, kv_sem, kv_recv, pair_sem, pair_recv, core_sem, core_recv, factor,
):
    me = lax.axis_index("ctx")
    z = lax.axis_index("tp")
    tokens, width = lg_hbm.shape
    columns = w_hbm.shape[0]
    heads = columns // HEAD
    half_heads = heads // 2
    chunks = lg_recv.shape[1]
    size = tokens // chunks
    large = chunks - 1
    small = fwd_sem.shape[0] - large
    sub = size // small
    ahead = 3
    pieces = far_sem.shape[0]
    quarter = columns // 4
    piece = quarter // pieces
    share = me % 4
    twin = me + 1 - 2 * (me % 2)
    core = me % 2
    pal = me + 2 - 4 * ((me // 2) % 2)
    pal_share = (share + 2) % 4
    is_end = (z == 0) | (z == 3)
    is_mid = (z == 1) | (z == 2)
    low = z // 2
    end = 3 * low
    mid = 1 + low
    mid2 = 2 - low
    end2 = 3 - end
    far_col = pl.multiple_of((1 - low) * 2 * width, 2 * width)
    near_col = pl.multiple_of(low * 2 * width, 2 * width)

    def col(part):
        return pl.ds(pl.multiple_of(part * width, width), width)

    def row(i):
        return pl.ds(pl.multiple_of(tokens - (i + 1) * size, size), size)

    def sub_row(j):
        return pl.ds(pl.multiple_of(size - (j + 1) * sub, sub), sub)

    barrier = pltpu.get_barrier_semaphore()
    for d in range(1, n_ctx):
        pl.semaphore_signal(barrier, inc=1, device_id=((me + d) % n_ctx, z), device_id_type=MESH)

    @pl.when(is_end)
    def _():
        pl.semaphore_signal(barrier, inc=1, device_id=(me, mid), device_id_type=MESH)
        pl.semaphore_wait(barrier, n_ctx)

    @pl.when(is_mid)
    def _():
        pl.semaphore_signal(barrier, inc=1, device_id=(me, end), device_id_type=MESH)
        pl.semaphore_signal(barrier, inc=1, device_id=(me, mid2), device_id_type=MESH)
        pl.semaphore_wait(barrier, n_ctx + 1)

    def remote(src, dst, send, recv, target):
        return pltpu.make_async_remote_copy(
            src_ref=src, dst_ref=dst, send_sem=send, recv_sem=recv, device_id=target, device_id_type=MESH)

    def lg_from_hbm(i, sems, target_z):
        return remote(lg_hbm.at[row(i), :], lg.at[row(i), col(z)], sems.at[i], lg_recv.at[z, i], (me, target_z))

    def lg_arrival(part, i):
        place = lg.at[row(i), col(part)]
        return remote(place, place, fwd_sem.at[0], lg_recv.at[part, i], (me, mid2))

    def forward(rows, n):
        place = lg.at[rows, col(end)]
        return remote(place, place, fwd_sem.at[n], end2_recv.at[n], (me, mid2))

    def end2_arrival(rows, n):
        place = lg.at[rows, col(end2)]
        return remote(place, place, fwd_sem.at[n], end2_recv.at[n], (me, mid2))

    def part_send(rows, n):
        return remote(part_out.at[rows, :], part_in.at[rows, :], part_sem.at[n], part_recv.at[n], (me, end))

    def each_row(step):
        @pl.loop(0, large)
        def _(i):
            step(row(i), i)

        @pl.loop(0, small)
        def _(j):
            step(sub_row(j), large + j)

    def far_rows(which, p):
        return pl.ds(pl.multiple_of(which * quarter + p * piece, piece), piece)

    def far_send(p):
        return remote(w_hbm.at[far_rows(share, p), pl.ds(far_col, 2 * width)], far.at[far_rows(share, p), :],
                      far_sem.at[p], far_recv.at[p], (me, mid))

    def far_share(which, p, slot, target):
        place = far.at[far_rows(which, p), :]
        return remote(place, place, twin_sem.at[slot, p], twin_recv.at[slot, p], (target, z))

    @pl.when(is_end)
    def _():
        for p in range(pieces):
            far_send(p).start()

        @pl.loop(0, chunks)
        def _(i):
            lg_from_hbm(i, ends_sem, mid).start()

    @pl.when(is_mid)
    def _():
        @pl.loop(0, chunks)
        def _(i):
            lg_from_hbm(i, mids_sem, mid2).start()
            lg_from_hbm(i, ends_sem, end).start()

    loads = [
        pltpu.make_async_copy(k_hbm, k_buf, load_sem.at[0]),
        pltpu.make_async_copy(v_hbm, v_buf, load_sem.at[1]),
        pltpu.make_async_copy(q_hbm, q_buf, load_sem.at[2]),
        pltpu.make_async_copy(lg_hbm, lg.at[:, col(z)], load_sem.at[3]),
        pltpu.make_async_copy(w_hbm, w, load_sem.at[4]),
    ]
    for load in loads:
        load.start()
    loads[0].wait()
    loads[1].wait()

    def head(h):
        return pl.ds(pl.multiple_of(h * HEAD, HEAD), HEAD)

    def by_head(step, first=0, count=heads, unroll=4):
        @pl.loop(0, count // unroll)
        def _(n):
            for u in range(unroll):
                step(first + n * unroll + u)

    def sum_kv(h):
        total = jnp.zeros((HEAD, HEAD), F32)
        for c, (start, length) in enumerate(spans):
            at = pl.ds(start, length)
            here = mm(v_buf[at, head(h)], k_buf[at, head(h)], TN)
            kv_sums[c, h] = here
            total = total + here
        kv_out[h] = total.astype(BF16)
        state[h] = jnp.zeros((HEAD, HEAD), F32)

    by_head(sum_kv, unroll=2)

    for d in range(1, n_ctx):
        @pl.when(me + d < n_ctx)
        def _():
            remote(kv_out, kv_in.at[d - 1], kv_sem.at[d - 1], kv_recv.at[d - 1], ((me + d) % n_ctx, z)).start()
    for load in loads[2:]:
        load.wait()

    def finish_kv():
        for d in range(1, n_ctx):
            @pl.when(me >= d)
            def _():
                remote(kv_in.at[d - 1], kv_in.at[d - 1], kv_sem.at[d - 1], kv_recv.at[d - 1], (twin, z)).wait_recv()

            @pl.when(me < d)
            def _():
                kv_in[d - 1] = jnp.zeros(kv_in.shape[1:], BF16)

        def total_kv(h):
            total = kv_in[0, h].astype(F32)
            for d in range(2, n_ctx):
                total = total + kv_in[d - 1, h].astype(F32)
            for c in reversed(range(len(spans))):
                kv_state[c, h] = total.astype(BF16)
                total = total + kv_sums[c, h]

        by_head(total_kv, unroll=2)

    def attend(c, start, length, keep):
        at = pl.ds(start, length)
        rows_at = lax.broadcasted_iota(jnp.int32, (length, length), 0)
        cols_at = lax.broadcasted_iota(jnp.int32, (length, length), 1)

        def step(h):
            hd = head(h)
            q, k, v, g = q_buf[at, hd], k_buf[at, hd], v_buf[at, hd], g_ref[at, hd]
            grad_rows = jnp.where(rows_at >= cols_at, mm(g, v, NT), 0.0).astype(BF16)
            grad_cols = jnp.where(rows_at <= cols_at, mm(v, g, NT), 0.0).astype(BF16)
            query_cols = jnp.where(rows_at <= cols_at, mm(k, q, NT), 0.0).astype(BF16)
            total = state[h]
            later = total.astype(BF16)
            query = mm(grad_rows, k, NN) + mm(g, kv_state[c, h], NN)
            qo_buf[at, hd] = (factor * query).astype(BF16)
            key_part[at, hd] = mm(grad_cols, q, NN) + mm(v, later, NT)
            value_part[at, hd] = mm(query_cols, g, NN) + mm(k, later, NN)
            if keep:
                state[h] = total + mm(q, g, TN)

        return step

    def attend_block(i):
        for c in range(len(spans) - 2):
            @pl.when(i == 2 * c + 2)
            def _():
                by_head(attend(c, *spans[c], True))

    def attend_part(j):
        c = len(spans) - 2
        for n in range(heads // 4):
            @pl.when(j == n + 1)
            def _():
                by_head(attend(c, *spans[c], True), 4 * n, 4)

    def project(left, right, out_ref, at, tile):
        @pl.loop(0, columns // tile)
        def _(n):
            out = pl.ds(pl.multiple_of(n * tile, tile), tile)
            out_ref[at, out] = mm(left[at, :], right[out, :], NT)

    near = pl.ds(near_col, 2 * width)
    middle = pl.ds(width, 2 * width)
    far_mid2 = pl.ds(pl.multiple_of(low * width, width), width)
    far_end2 = pl.ds(pl.multiple_of((1 - low) * width, width), width)
    tile = 512
    block = 2 * size
    blocks = tokens // block

    def span(c):
        return pl.ds(pl.multiple_of(tokens - (c + 1) * block, block), block)

    @pl.when(is_end)
    def _():
        @pl.loop(0, blocks)
        def _(c):
            for j in range(2):
                lg_arrival(mid, c * 2 + j).wait_recv()
            project(lg.at[:, near], w.at[:, near], key_part, span(c), tile)

        finish_kv()

        def take(rows, n):
            part_send(rows, n).wait_recv()
            g_ref[rows, :] = (key_part[rows, :] + part_in[rows, :].astype(F32)).astype(BF16)

        @pl.loop(0, large)
        def _(i):
            attend_block(i)
            take(row(i), i)

        @pl.loop(0, small)
        def _(j):
            attend_part(j)
            take(sub_row(j), large + j)

    @pl.when(is_mid)
    def _():
        for c in range(blocks):
            for j in range(2):
                lg_arrival(mid2, c * 2 + j).wait_recv()
            if c < pieces:
                far_send(c).wait_recv()
                far_share(share, c, 0, pal).start()
                far_share(share, c, 1, twin).start()
            if c == pieces:
                for p in range(pieces):
                    far_share(pal_share, p, 0, pal).wait_recv()
                    far_share(pal_share, p, 2, twin).start()
            for i in {2: range(1), 3: range(1, ahead)}.get(c, ()):
                lg_arrival(end, i).wait_recv()
                forward(row(i), i).start()
            project(lg.at[:, middle], w.at[:, middle], key_part, span(c), tile)
        finish_kv()
        for p in range(pieces):
            far_share(share + 1 - 2 * core, p, 1, twin).wait_recv()
            far_share(pal_share + 1 - 2 * core, p, 2, twin).wait_recv()

        @pl.loop(0, blocks)
        def _(c):
            project(lg.at[:, col(mid2)], far.at[:, far_mid2], value_part, span(c), tile)

        def give(rows, n):
            end2_arrival(rows, n).wait_recv()
            total = value_part[rows, :] + mm(lg[rows, col(end2)], far[:, far_end2], NT)
            part_out[rows, :] = total.astype(BF16)
            part_send(rows, n).start()

        def own(rows, step):
            @pl.loop(0, columns // step)
            def _(n):
                out = pl.ds(pl.multiple_of(n * step, step), step)
                total = key_part[rows, out] + mm(lg[rows, col(end)], w[out, col(end)], NT)
                g_ref[rows, out] = (total + mm(lg[rows, col(end2)], w[out, col(end2)], NT)).astype(BF16)

        @pl.loop(0, large)
        def _(i):
            @pl.when(i < large - ahead)
            def _():
                lg_arrival(end, i + ahead).wait_recv()
                forward(row(i + ahead), i + ahead).start()

            @pl.when(i == large - ahead)
            def _():
                lg_arrival(end, large).wait_recv()
                for j in range(small):
                    forward(sub_row(j), large + j).start()

            attend_block(i)
            give(row(i), i)

            @pl.when(i % 2 == 1)
            def _():
                own(span(i // 2), tile)

            @pl.when(i == large - 1)
            def _():
                own(row(large - 1), columns)

        @pl.loop(0, small)
        def _(j):
            attend_part(j)
            give(sub_row(j), large + j)

        own(pl.ds(0, size), columns)

    chip = me // 2
    n_chips = n_ctx // 2
    mine = pl.ds(pl.multiple_of(core * half_heads, half_heads), half_heads)
    other = pl.ds(pl.multiple_of((1 - core) * half_heads, half_heads), half_heads)
    swap = remote(grad_out.at[other], grad_twin.at[other], core_sem.at[0], core_recv.at[0], (twin, z))
    swap_in = remote(grad_out.at[mine], grad_twin.at[mine], core_sem.at[0], core_recv.at[0], (twin, z))
    extra = remote(grad_out.at[mine], grad_twin.at[mine], core_sem.at[1], core_recv.at[1], (twin, z))
    extra_in = remote(grad_out.at[other], grad_twin.at[other], core_sem.at[1], core_recv.at[1], (twin, z))
    final = len(spans) - 1
    last_rows = pl.ds(*spans[final])

    def sum_grad(h):
        total = state[h] + mm(q_buf[last_rows, head(h)], g_ref[last_rows, head(h)], TN)
        after[h] = total
        grad_out[h] = total.astype(BF16)

    by_head(sum_grad, (1 - core) * half_heads, half_heads)
    swap.start()
    by_head(sum_grad, core * half_heads, half_heads)

    @pl.when(core == 1)
    def _():
        extra.start()

    swap_in.wait_recv()

    def make_pair(j):
        h = core * half_heads + j
        pair[j] = (after[h] + grad_twin[h].astype(F32)).astype(BF16)

    by_head(make_pair, 0, half_heads)

    def pair_copy(d):
        return remote(pair, pair_in.at[d - 1], pair_sem.at[d - 1], pair_recv.at[d - 1],
                      ((me + n_ctx - 2 * d) % n_ctx, z))

    for d in reversed(range(1, n_chips)):
        @pl.when(chip >= d)
        def _():
            pair_copy(d).start()

    by_head(attend(final, *spans[final], False))

    for d in range(1, n_chips):
        @pl.when(chip + d < n_chips)
        def _():
            pair_copy(d).wait_recv()

        @pl.when(chip + d >= n_chips)
        def _():
            pair_in[d - 1] = jnp.zeros(pair_in.shape[1:], BF16)

    def sum_rest(j):
        total = pair_in[0, j].astype(F32)
        for d in range(2, n_chips):
            total = total + pair_in[d - 1, j].astype(F32)
        rest[j] = total

    by_head(sum_rest, 0, half_heads)
    last = remote(rest, rest_in, core_sem.at[2], core_recv.at[2], (twin, z))
    last.start()

    @pl.when(core == 0)
    def _():
        extra_in.wait_recv()

    def finish_grad(j, ref, first):
        total = ref[j] + jnp.where(core == 0, grad_twin[first + j].astype(F32), 0.0)
        grad_after[first + j] = total.astype(BF16)

    by_head(lambda j: finish_grad(j, rest, core * half_heads), 0, half_heads)
    last.wait_recv()
    by_head(lambda j: finish_grad(j, rest_in, (1 - core) * half_heads), 0, half_heads)

    swap.wait_send()
    last.wait_send()

    @pl.when(core == 1)
    def _():
        extra.wait_send()

    for d in range(1, n_ctx):
        @pl.when(me + d < n_ctx)
        def _():
            remote(kv_out, kv_in.at[d - 1], kv_sem.at[d - 1], kv_recv.at[d - 1], (twin, z)).wait_send()

    for d in range(1, n_chips):
        @pl.when(chip >= d)
        def _():
            pair_copy(d).wait_send()

    @pl.when(is_end)
    def _():
        for p in range(pieces):
            far_send(p).wait_send()

        @pl.loop(0, chunks)
        def _(i):
            lg_from_hbm(i, ends_sem, mid).wait_send()

    @pl.when(is_mid)
    def _():
        for p in range(pieces):
            far_share(share, p, 0, pal).wait_send()
            far_share(share, p, 1, twin).wait_send()
            far_share(pal_share, p, 2, twin).wait_send()

        @pl.loop(0, chunks)
        def _(i):
            lg_from_hbm(i, ends_sem, end).wait_send()
            lg_from_hbm(i, mids_sem, mid2).wait_send()

        each_row(lambda rows, n: forward(rows, n).wait_send())
        each_row(lambda rows, n: part_send(rows, n).wait_send())


def finish_kernel(factor, qo_buf, key_part, value_part, grad_after, k_buf, v_buf, qo, ko, vo, ko_buf, vo_buf, sem):
    heads = grad_after.shape[0]
    group = 2
    query_out = pltpu.make_async_copy(qo_buf, qo, sem.at[0, 0])
    query_out.start()

    def columns(n):
        return pl.ds(pl.multiple_of(n * group * HEAD, group * HEAD), group * HEAD)

    def key_out(n):
        return pltpu.make_async_copy(ko_buf.at[:, columns(n)], ko.at[:, columns(n)], sem.at[1, n])

    def value_out(n):
        return pltpu.make_async_copy(vo_buf.at[:, columns(n)], vo.at[:, columns(n)], sem.at[2, n])

    @pl.loop(0, heads // group)
    def _(n):
        for u in range(group):
            h = n * group + u
            at = pl.ds(pl.multiple_of(h * HEAD, HEAD), HEAD)
            after = grad_after[h]
            ko_buf[:, at] = (factor * (key_part[:, at] + mm(v_buf[:, at], after, NT))).astype(BF16)
            vo_buf[:, at] = (factor * (value_part[:, at] + mm(k_buf[:, at], after, NN))).astype(BF16)
        key_out(n).start()
        value_out(n).start()

    query_out.wait()

    @pl.loop(0, heads // group)
    def _(n):
        key_out(n).wait()
        value_out(n).wait()


def fused(q, k, v, lg, w, n_ctx, factor):
    tokens, width = lg.shape
    columns = w.shape[0]
    heads = columns // HEAD
    chunks = 8
    small = 4
    pieces = 2
    size = tokens // chunks
    spans = [(tokens - (c + 1) * 2 * size, 2 * size) for c in range(chunks // 2 - 1)] + [(size, size), (0, size)]
    n_spans = len(spans)
    stream = chunks - 1 + small
    dma = pltpu.SemaphoreType.DMA
    vmem = pltpu.VMEM
    state = (heads, HEAD, HEAD)
    half = (heads // 2, HEAD, HEAD)
    whole = (tokens, columns)
    chips = n_ctx // 2
    any_spec = pl.BlockSpec(memory_space=pl.ANY)
    vmem_spec = pl.BlockSpec(memory_space=pltpu.VMEM)
    parts = pl.pallas_call(
        functools.partial(gather_kernel, n_ctx, spans, factor=factor),
        out_shape=[vmem(whole, BF16), vmem(whole, F32), vmem(whole, F32), vmem(state, BF16), vmem(whole, BF16), vmem(whole, BF16)],
        in_specs=[any_spec] * 5,
        out_specs=[vmem_spec] * 6,
        scratch_shapes=[
            vmem(whole, BF16), vmem(whole, BF16),
            vmem((tokens, 4 * width), BF16), vmem(w.shape, BF16), vmem((columns, 2 * width), BF16),
            vmem(whole, BF16), vmem(whole, BF16),
            vmem((n_spans,) + state, F32), vmem((n_spans,) + state, BF16), vmem(state, F32), vmem(state, F32),
            vmem(state, BF16), vmem((n_ctx - 1,) + state, BF16), vmem(state, BF16), vmem(state, BF16),
            vmem(half, BF16), vmem((chips - 1,) + half, BF16), vmem(half, F32), vmem(half, F32),
            dma((5,)), dma((chunks,)), dma((chunks,)), dma((4, chunks)), dma((stream,)), dma((stream,)),
            dma((stream,)), dma((stream,)),
            dma((pieces,)), dma((pieces,)), dma((3, pieces)), dma((3, pieces)),
            dma((n_ctx - 1,)), dma((n_ctx - 1,)), dma((chips - 1,)), dma((chips - 1,)),
            dma((3,)), dma((3,)),
        ],
        compiler_params=pltpu.CompilerParams(
            collective_id=0, has_side_effects=True, vmem_limit_bytes=44 * 1024 * 1024),
    )(q, k, v, lg, w)
    return pl.pallas_call(
        functools.partial(finish_kernel, factor),
        out_shape=[jax.ShapeDtypeStruct(whole, BF16)] * 3,
        in_specs=[vmem_spec] * 6,
        out_specs=[any_spec] * 3,
        scratch_shapes=[vmem(whole, BF16), vmem(whole, BF16), dma((3, heads // 2))],
        compiler_params=pltpu.CompilerParams(vmem_limit_bytes=24 * 1024 * 1024),
    )(*parts)


def gather_plain(q, k, v, lg, w):
    tokens, columns = q.shape
    heads = columns // HEAD
    me = lax.axis_index("ctx")
    g = lax.dot_general(lax.all_gather(lg, "tp", axis=1, tiled=True), w, NT, preferred_element_type=F32).astype(BF16)
    three = (tokens, heads, HEAD)
    kv_here = jnp.einsum("lbg,lbz->bgz", k.reshape(three), v.reshape(three), preferred_element_type=F32)
    grad_here = jnp.einsum("lbg,lbz->bgz", q.reshape(three), g.reshape(three), preferred_element_type=F32)

    def pick(mine, lower):
        stacked = lax.all_gather(mine[None], "ctx", axis=0, tiled=True)
        index = jnp.arange(stacked.shape[0])
        chosen = index < me if lower else index > me
        return jnp.sum(jnp.where(chosen[:, None, None, None], stacked, 0.0), 0).astype(BF16)

    return g, pick(kv_here, True), pick(grad_here, False)


def local(q, k, v, lg, w):
    n_ctx = lax.axis_size("ctx")
    n_tp = lax.axis_size("tp")
    factor = float((HEAD * q.shape[0] * n_ctx) ** (-0.5))
    if n_tp == 4 and n_ctx == 8 and q.shape[0] % 1024 == 0 and q.shape[1] % 1024 == 0:
        return tuple(fused(q, k, v, lg, w, n_ctx, factor))
    g, kv_before, grad_after = gather_plain(q, k, v, lg, w)
    return tuple(attention(q, k, v, g, kv_before, grad_after, factor))


def solution(mesh):
    return jax.shard_map(
        local,
        mesh=mesh,
        in_specs=(P("ctx", "tp"), P("ctx", "tp"), P("ctx", "tp"), P("ctx", "tp"), P("tp", None)),
        out_specs=(P("ctx", "tp"), P("ctx", "tp"), P("ctx", "tp")),
        check_vma=False,
    )
```

```python
import functools

import jax
import jax.numpy as jnp
from jax import lax
from jax.experimental import pallas as pl
from jax.experimental.pallas import tpu as pltpu
from jax.sharding import PartitionSpec as P

HEAD = 128
MESH = pl.DeviceIdType.MESH
F32 = jnp.float32
BF16 = jnp.bfloat16
NT = (((1,), (1,)), ((), ()))
NN = (((1,), (0,)), ((), ()))
TN = (((0,), (0,)), ((), ()))


def mm(a, b, dims):
    return lax.dot_general(a, b, dims, preferred_element_type=F32)


def attention_head(read, state_kv, state_grad, write, tokens, size, factor):
    count = tokens // size
    pieces = [read(i) for i in range(count)]
    rows = lax.broadcasted_iota(jnp.int32, (size, size), 0)
    cols = lax.broadcasted_iota(jnp.int32, (size, size), 1)
    causal = rows >= cols
    after = [None] * count
    total = state_grad
    for i in reversed(range(count)):
        after[i] = total.astype(BF16)
        if i:
            q, _, _, g = pieces[i]
            total = total + mm(q, g, TN)
    before = state_kv
    for i in range(count):
        q, k, v, g = pieces[i]
        inner_grad = jnp.where(causal, mm(g, v, NT), 0.0).astype(BF16)
        inner_query = jnp.where(causal, mm(q, k, NT), 0.0).astype(BF16)
        query = mm(inner_grad, k, NN) + mm(g, before.astype(BF16), NT)
        key = mm(inner_grad, q, TN) + mm(v, after[i], NT)
        value = mm(inner_query, g, TN) + mm(k, after[i], NN)
        write(i, (factor * query).astype(BF16), (factor * key).astype(BF16), (factor * value).astype(BF16))
        if i < count - 1:
            before = before + mm(k, v, TN)


def attention_kernel(size, factor, q_ref, k_ref, v_ref, g_ref, kv_ref, grad_ref, qo_ref, ko_ref, vo_ref):
    tokens = q_ref.shape[0]

    def read(i):
        at = pl.ds(i * size, size)
        return q_ref[at, :], k_ref[at, :], v_ref[at, :], g_ref[at, :]

    def write(i, query, key, value):
        at = pl.ds(i * size, size)
        qo_ref[at, :] = query
        ko_ref[at, :] = key
        vo_ref[at, :] = value

    attention_head(read, kv_ref[0].astype(F32), grad_ref[0].astype(F32), write, tokens, size, factor)


def attention(q, k, v, g, kv_before, grad_after, factor):
    tokens, columns = q.shape
    size = min(256, tokens)
    rows = pl.BlockSpec((tokens, HEAD), lambda h: (0, h))
    state = pl.BlockSpec((1, HEAD, HEAD), lambda h: (h, 0, 0))
    return pl.pallas_call(
        functools.partial(attention_kernel, size, factor),
        grid=(columns // HEAD,),
        out_shape=[jax.ShapeDtypeStruct(q.shape, BF16)] * 3,
        in_specs=[rows] * 4 + [state] * 2,
        out_specs=[rows] * 3,
    )(q, k, v, g, kv_before, grad_after)


def gather_kernel(
    n_ctx, spans, q_hbm, k_hbm, v_hbm, lg_hbm, w_hbm, qo_buf, ko_buf, vo_buf, key_part, value_part, grad_after, k_buf, v_buf,
    q_buf, g_ref, lg, w, far, part_out, part_in,
    kv_sums, kv_state, state, after, kv_bufs, grad_bufs,
    load_sem, ends_sem, mids_sem, outs_sem, end_recv, mid_recv, out_recv, fwd_sem, end2_recv, part_sem, part_recv,
    far_sem, far_recv, twin_sem, twin_recv, factor,
):
    me = lax.axis_index("ctx")
    z = lax.axis_index("tp")
    tokens, width = lg_hbm.shape
    columns = w_hbm.shape[0]
    heads = columns // HEAD
    half_heads = heads // 2
    part_heads = half_heads // 2
    chunks = ends_sem.shape[0]
    size = tokens // chunks
    small = fwd_sem.shape[0] // chunks
    sub = size // small
    ahead = 3
    pieces = far_sem.shape[0]
    quarter = columns // 4
    piece = quarter // pieces
    share = me % 4
    twin = me + 1 - 2 * (me % 2)
    core = me % 2
    pal = me + 2 - 4 * ((me // 2) % 2)
    pal_share = (share + 2) % 4
    is_end = (z == 0) | (z == 3)
    is_mid = (z == 1) | (z == 2)
    low = z // 2
    end = 3 * low
    mid = 1 + low
    mid2 = 2 - low
    end2 = 3 - end
    far_col = pl.multiple_of((1 - low) * 2 * width, 2 * width)
    near_col = pl.multiple_of(low * 2 * width, 2 * width)

    def col(part):
        return pl.ds(pl.multiple_of(part * width, width), width)

    def row(i):
        return pl.ds(pl.multiple_of(tokens - (i + 1) * size, size), size)

    def sub_row(i, j):
        return pl.ds(pl.multiple_of(tokens - i * size - (j + 1) * sub, sub), sub)

    barrier = pltpu.get_barrier_semaphore()
    for d in range(1, n_ctx):
        pl.semaphore_signal(barrier, inc=1, device_id=((me + d) % n_ctx, z), device_id_type=MESH)

    @pl.when(is_end)
    def _():
        pl.semaphore_signal(barrier, inc=1, device_id=(me, mid), device_id_type=MESH)
        pl.semaphore_wait(barrier, n_ctx)

    @pl.when(is_mid)
    def _():
        pl.semaphore_signal(barrier, inc=1, device_id=(me, end), device_id_type=MESH)
        pl.semaphore_signal(barrier, inc=1, device_id=(me, mid2), device_id_type=MESH)
        pl.semaphore_wait(barrier, n_ctx + 1)

    def remote(src, dst, send, recv, target):
        return pltpu.make_async_remote_copy(
            src_ref=src, dst_ref=dst, send_sem=send, recv_sem=recv, device_id=target, device_id_type=MESH)

    def end_copy(i):
        return remote(lg_hbm.at[row(i), :], lg.at[row(i), col(end)], ends_sem.at[i], end_recv.at[i], (me, mid))

    def mid_copy(i, part):
        return remote(lg_hbm.at[row(i), :], lg.at[row(i), col(part)], mids_sem.at[i], mid_recv.at[i], (me, mid2))

    def out_copy(i, part):
        return remote(lg_hbm.at[row(i), :], lg.at[row(i), col(part)], outs_sem.at[i], out_recv.at[i], (me, end))

    def forward(rows, n):
        place = lg.at[rows, col(end)]
        return remote(place, place, fwd_sem.at[n], end2_recv.at[n], (me, mid2))

    def end2_arrival(rows, n):
        place = lg.at[rows, col(end2)]
        return remote(place, place, fwd_sem.at[n], end2_recv.at[n], (me, mid2))

    def part_send(rows, n):
        return remote(part_out.at[rows, :], part_in.at[rows, :], part_sem.at[n], part_recv.at[n], (me, end))

    def chunk_rows(i, step):
        @pl.loop(0, small)
        def _(j):
            step(sub_row(i, j), i * small + j)

    def each_row(step):
        @pl.loop(0, chunks)
        def _(i):
            chunk_rows(i, step)

    def far_rows(which, p):
        return pl.ds(pl.multiple_of(which * quarter + p * piece, piece), piece)

    def far_send(p):
        return remote(w_hbm.at[far_rows(share, p), pl.ds(far_col, 2 * width)], far.at[far_rows(share, p), :],
                      far_sem.at[p], far_recv.at[p], (me, mid))

    def far_share(which, p, slot, target):
        place = far.at[far_rows(which, p), :]
        return remote(place, place, twin_sem.at[slot, p], twin_recv.at[slot, p], (target, z))

    @pl.when(is_end)
    def _():
        for p in range(pieces):
            far_send(p).start()

        @pl.loop(0, chunks)
        def _(i):
            end_copy(i).start()

    @pl.when(is_mid)
    def _():
        @pl.loop(0, chunks)
        def _(i):
            mid_copy(i, mid).start()
            out_copy(i, mid).start()

    loads = [
        pltpu.make_async_copy(k_hbm, k_buf, load_sem.at[0]),
        pltpu.make_async_copy(v_hbm, v_buf, load_sem.at[1]),
        pltpu.make_async_copy(q_hbm, q_buf, load_sem.at[2]),
        pltpu.make_async_copy(lg_hbm, lg.at[:, col(z)], load_sem.at[3]),
        pltpu.make_async_copy(w_hbm, w, load_sem.at[4]),
    ]
    for load in loads:
        load.start()
    loads[0].wait()
    loads[1].wait()

    def head(h):
        return pl.ds(pl.multiple_of(h * HEAD, HEAD), HEAD)

    def by_head(step, first=0, count=heads, unroll=4):
        @pl.loop(0, count // unroll)
        def _(n):
            for u in range(unroll):
                step(first + n * unroll + u)

    chip = me // 2
    n_chips = n_ctx // 2
    mine = pl.ds(pl.multiple_of(core * half_heads, half_heads), half_heads)
    other = pl.ds(pl.multiple_of((1 - core) * half_heads, half_heads), half_heads)

    class Exchange:
        def __init__(self, bufs, down):
            (self.out, self.twin, self.pair, self.pair_in, self.rest, self.rest_in,
             self.core_sem, self.core_recv, self.pair_sem, self.pair_recv) = bufs
            self.down = down
            self.giver = 1 if down else 0

        def core_copy(self, src, dst, n):
            return remote(src, dst, self.core_sem.at[n], self.core_recv.at[n], (twin, z))

        def swap(self, first, n):
            at = pl.ds(first + n * part_heads, part_heads)
            return self.core_copy(self.out.at[at], self.twin.at[at], n)

        def extra(self, heads_at):
            return self.core_copy(self.out.at[heads_at], self.twin.at[heads_at], 2)

        def last(self, n):
            at = pl.ds(n * part_heads, part_heads)
            return self.core_copy(self.rest.at[at], self.rest_in.at[at], 3 + n)

        def pair_copy(self, d, n):
            target = me + n_ctx - 2 * d if self.down else me + 2 * d
            at = pl.ds(n * part_heads, part_heads)
            return remote(self.pair.at[at], self.pair_in.at[d - 1, at], self.pair_sem.at[d - 1, n],
                          self.pair_recv.at[d - 1, n], (target % n_ctx, z))

        def sends(self, d):
            return chip >= d if self.down else chip + d < n_chips

        def takes(self, d):
            return chip + d < n_chips if self.down else chip >= d

        def begin(self, total):
            def step(h):
                value = total(h)
                after[h] = value
                self.out[h] = value.astype(BF16)

            for n in range(2):
                by_head(step, (1 - core) * half_heads + n * part_heads, part_heads, 2)
                self.swap((1 - core) * half_heads, n).start()
            by_head(step, core * half_heads, half_heads)

            @pl.when(core == self.giver)
            def _():
                self.extra(mine).start()

        def combine(self):
            def step(j):
                h = core * half_heads + j
                self.pair[j] = (after[h] + self.twin[h].astype(F32)).astype(BF16)

            for n in range(2):
                self.swap(core * half_heads, n).wait_recv()
                by_head(step, n * part_heads, part_heads, 2)
                for d in reversed(range(1, n_chips)):
                    @pl.when(self.sends(d))
                    def _():
                        self.pair_copy(d, n).start()

        def collect(self):
            def step(j):
                total = self.pair_in[0, j].astype(F32)
                for d in range(2, n_chips):
                    total = total + self.pair_in[d - 1, j].astype(F32)
                self.rest[j] = total

            for n in range(2):
                for d in range(1, n_chips):
                    @pl.when(self.takes(d))
                    def _():
                        self.pair_copy(d, n).wait_recv()

                    @pl.when(jnp.logical_not(self.takes(d)))
                    def _():
                        at = pl.ds(n * part_heads, part_heads)
                        self.pair_in[d - 1, at] = jnp.zeros((part_heads, HEAD, HEAD), BF16)

                by_head(step, n * part_heads, part_heads, 2)
                self.last(n).start()

        def finish(self, write, between):
            @pl.when(core != self.giver)
            def _():
                self.extra(other).wait_recv()

            def step(j, ref, first):
                own = jnp.where(core != self.giver, self.twin[first + j].astype(F32), 0.0)
                write(first + j, ref[j] + own)

            by_head(lambda j: step(j, self.rest, core * half_heads), 0, half_heads)
            between()
            for n in range(2):
                self.last(n).wait_recv()
            by_head(lambda j: step(j, self.rest_in, (1 - core) * half_heads), 0, half_heads)

        def drain(self):
            @pl.when(core == self.giver)
            def _():
                self.extra(mine).wait_send()

            for n in range(2):
                self.swap((1 - core) * half_heads, n).wait_send()
                self.last(n).wait_send()
                for d in range(1, n_chips):
                    @pl.when(self.sends(d))
                    def _():
                        self.pair_copy(d, n).wait_send()

    kv = Exchange(kv_bufs, False)
    grad = Exchange(grad_bufs, True)

    def sum_kv(h):
        total = jnp.zeros((HEAD, HEAD), F32)
        for c, (start, length) in enumerate(spans):
            at = pl.ds(start, length)
            here = mm(v_buf[at, head(h)], k_buf[at, head(h)], TN)
            kv_sums[c, h] = here
            total = total + here
        state[h] = jnp.zeros((HEAD, HEAD), F32)
        return total

    kv.begin(sum_kv)
    kv.combine()
    for load in loads[2:]:
        load.wait()

    def set_kv(h, total):
        for c in reversed(range(len(spans))):
            kv_state[c, h] = total.astype(BF16)
            total = total + kv_sums[c, h]

    def attend(c, start, length, keep):
        at = pl.ds(start, length)
        rows_at = lax.broadcasted_iota(jnp.int32, (length, length), 0)
        cols_at = lax.broadcasted_iota(jnp.int32, (length, length), 1)

        def step(h):
            hd = head(h)
            q, k, v, g = q_buf[at, hd], k_buf[at, hd], v_buf[at, hd], g_ref[at, hd]
            grad_rows = jnp.where(rows_at >= cols_at, mm(g, v, NT), 0.0).astype(BF16)
            grad_cols = jnp.where(rows_at <= cols_at, mm(v, g, NT), 0.0).astype(BF16)
            query_cols = jnp.where(rows_at <= cols_at, mm(k, q, NT), 0.0).astype(BF16)
            total = state[h]
            later = total.astype(BF16)
            query = mm(grad_rows, k, NN) + mm(g, kv_state[c, h], NN)
            qo_buf[at, hd] = (factor * query).astype(BF16)
            key_part[at, hd] = mm(grad_cols, q, NN) + mm(v, later, NT)
            value_part[at, hd] = mm(query_cols, g, NN) + mm(k, later, NN)
            if keep:
                state[h] = total + mm(q, g, TN)

        return step

    def attend_some(n):
        share_of = max(1, heads // (2 * small))
        for c in range(len(spans) - 1):
            @pl.when((n >= 2 * small * (c + 1)) & (n < 2 * small * (c + 2)))
            def _():
                first = (n - 2 * small * (c + 1)) * share_of
                by_head(attend(c, *spans[c], True), first, share_of, share_of)

    def project(left, right, out_ref, at, tile):
        @pl.loop(0, columns // tile)
        def _(n):
            out = pl.ds(pl.multiple_of(n * tile, tile), tile)
            out_ref[at, out] = mm(left[at, :], right[out, :], NT)

    middle = pl.ds(width, 2 * width)
    near = pl.ds(near_col, 2 * width)
    far_mid2 = pl.ds(pl.multiple_of(low * width, width), width)
    far_end2 = pl.ds(pl.multiple_of((1 - low) * width, width), width)
    tile = 512
    block = 2 * size
    blocks = tokens // block

    def span(c):
        return pl.ds(pl.multiple_of(tokens - (c + 1) * block, block), block)

    @pl.when(is_end)
    def _():
        @pl.loop(0, blocks)
        def _(c):
            for j in range(2):
                out_copy(c * 2 + j, mid).wait_recv()
            project(lg.at[:, near], w.at[:, near], key_part, span(c), tile)

        kv.collect()
        kv.finish(set_kv, lambda: None)

        def take(rows, n):
            part_send(rows, n).wait_recv()
            g_ref[rows, :] = (key_part[rows, :] + part_in[rows, :].astype(F32)).astype(BF16)

        @pl.loop(0, chunks)
        def _(i):
            def step(rows, n):
                attend_some(n)
                take(rows, n)

            chunk_rows(i, step)

    @pl.when(is_mid)
    def _():
        def forward_chunk(i):
            end_copy(i).wait_recv()
            chunk_rows(i, lambda rows, n: forward(rows, n).start())

        for c in range(blocks):
            if c == 3:
                for i in range(1, ahead):
                    forward_chunk(i)
                kv.finish(set_kv, lambda: None)
                for p in range(pieces):
                    far_share(share + 1 - 2 * core, p, 1, twin).wait_recv()
                    far_share(pal_share + 1 - 2 * core, p, 2, twin).wait_recv()

                @pl.loop(0, c)
                def _(n):
                    project(lg.at[:, col(mid2)], far.at[:, far_mid2], value_part, span(n), tile)
            for j in range(2):
                mid_copy(c * 2 + j, mid2).wait_recv()
            if c < pieces:
                far_send(c).wait_recv()
                far_share(share, c, 0, pal).start()
                far_share(share, c, 1, twin).start()
            if c == 2:
                for p in range(pieces):
                    far_share(pal_share, p, 0, pal).wait_recv()
                    far_share(pal_share, p, 2, twin).start()
                kv.collect()
                forward_chunk(0)
            project(lg.at[:, middle], w.at[:, middle], key_part, span(c), tile)
        project(lg.at[:, col(mid2)], far.at[:, far_mid2], value_part, span(blocks - 1), tile)

        def give(rows, n):
            end2_arrival(rows, n).wait_recv()
            total = value_part[rows, :] + mm(lg[rows, col(end2)], far[:, far_end2], NT)
            part_out[rows, :] = total.astype(BF16)
            part_send(rows, n).start()

        def own(rows, step):
            @pl.loop(0, columns // step)
            def _(n):
                out = pl.ds(pl.multiple_of(n * step, step), step)
                total = key_part[rows, out] + mm(lg[rows, col(end)], w[out, col(end)], NT)
                g_ref[rows, out] = (total + mm(lg[rows, col(end2)], w[out, col(end2)], NT)).astype(BF16)

        @pl.loop(0, chunks)
        def _(i):
            @pl.when(i < chunks - ahead)
            def _():
                forward_chunk(i + ahead)

            def step(rows, n):
                attend_some(n)
                give(rows, n)

            chunk_rows(i, step)

            @pl.when(i % 2 == 1)
            def _():
                own(span(i // 2), tile)

    final = len(spans) - 1
    last_rows = pl.ds(*spans[final])
    grad.begin(lambda h: state[h] + mm(q_buf[last_rows, head(h)], g_ref[last_rows, head(h)], TN))
    grad.combine()
    by_head(attend(final, *spans[final], False))
    grad.collect()

    def set_grad(h, total):
        grad_after[h] = total.astype(BF16)

    def finish_half():
        by_head(lambda h: finish_head(factor, h, h, key_part, value_part, grad_after, k_buf, v_buf, ko_buf, vo_buf),
                core * half_heads, half_heads, 2)

    grad.finish(set_grad, finish_half)
    kv.drain()
    grad.drain()

    @pl.when(is_end)
    def _():
        for p in range(pieces):
            far_send(p).wait_send()

        @pl.loop(0, chunks)
        def _(i):
            end_copy(i).wait_send()

    @pl.when(is_mid)
    def _():
        for p in range(pieces):
            far_share(share, p, 0, pal).wait_send()
            far_share(share, p, 1, twin).wait_send()
            far_share(pal_share, p, 2, twin).wait_send()

        @pl.loop(0, chunks)
        def _(i):
            mid_copy(i, mid).wait_send()
            out_copy(i, mid).wait_send()

        each_row(lambda rows, n: forward(rows, n).wait_send())
        each_row(lambda rows, n: part_send(rows, n).wait_send())


def finish_kernel(
    factor, qo_buf, ko_half, vo_half, key_part, value_part, grad_after, k_buf, v_buf, qo, ko, vo, ko_buf, vo_buf, sem,
):
    heads = grad_after.shape[0]
    group = 2
    half = heads // 2
    core = lax.axis_index("ctx") % 2
    done = pl.ds(pl.multiple_of(core * half * HEAD, half * HEAD), half * HEAD)
    ready = [
        pltpu.make_async_copy(ko_half.at[:, done], ko.at[:, done], sem.at[1, 0]),
        pltpu.make_async_copy(vo_half.at[:, done], vo.at[:, done], sem.at[2, 0]),
        pltpu.make_async_copy(qo_buf, qo, sem.at[0, 0]),
    ]
    for copy in ready:
        copy.start()

    def copies(n):
        here = pl.ds(pl.multiple_of(n * group * HEAD, group * HEAD), group * HEAD)
        there = pl.ds(pl.multiple_of(((1 - core) * half + n * group) * HEAD, group * HEAD), group * HEAD)
        return (
            pltpu.make_async_copy(ko_buf.at[:, here], ko.at[:, there], sem.at[1, n + 1]),
            pltpu.make_async_copy(vo_buf.at[:, here], vo.at[:, there], sem.at[2, n + 1]),
        )

    for n in range(half // group):
        for u in range(group):
            to = n * group + u
            finish_head(factor, (1 - core) * half + to, to, key_part, value_part, grad_after, k_buf, v_buf, ko_buf, vo_buf)
        for copy in copies(n):
            copy.start()
    for copy in ready:
        copy.wait()
    for n in range(half // group):
        for copy in copies(n):
            copy.wait()


def finish_head(factor, h, to, key_part, value_part, grad_after, k_buf, v_buf, ko_buf, vo_buf):
    at = pl.ds(pl.multiple_of(h * HEAD, HEAD), HEAD)
    out = pl.ds(pl.multiple_of(to * HEAD, HEAD), HEAD)
    after = grad_after[h]
    ko_buf[:, out] = (factor * (key_part[:, at] + mm(v_buf[:, at], after, NT))).astype(BF16)
    vo_buf[:, out] = (factor * (value_part[:, at] + mm(k_buf[:, at], after, NN))).astype(BF16)


def fused(q, k, v, lg, w, n_ctx, factor):
    tokens, width = lg.shape
    columns = w.shape[0]
    heads = columns // HEAD
    chunks = 8
    small = 2
    pieces = 2
    size = tokens // chunks
    spans = [(tokens - (c + 1) * 2 * size, 2 * size) for c in range(chunks // 2)]
    n_spans = len(spans)
    stream = chunks * small
    dma = pltpu.SemaphoreType.DMA
    vmem = pltpu.VMEM
    state = (heads, HEAD, HEAD)
    half = (heads // 2, HEAD, HEAD)
    whole = (tokens, columns)
    chips = n_ctx // 2
    bufs = (
        vmem(state, BF16), vmem(state, BF16), vmem(half, BF16), vmem((chips - 1,) + half, BF16), vmem(half, F32), vmem(half, F32),
        dma((5,)), dma((5,)), dma((chips - 1, 2)), dma((chips - 1, 2)),
    )
    any_spec = pl.BlockSpec(memory_space=pl.ANY)
    vmem_spec = pl.BlockSpec(memory_space=pltpu.VMEM)
    parts = pl.pallas_call(
        functools.partial(gather_kernel, n_ctx, spans, factor=factor),
        out_shape=[
            vmem(whole, BF16), vmem(whole, BF16), vmem(whole, BF16), vmem(whole, F32), vmem(whole, F32), vmem(state, BF16),
            vmem(whole, BF16), vmem(whole, BF16),
        ],
        in_specs=[any_spec] * 5,
        out_specs=[vmem_spec] * 8,
        scratch_shapes=[
            vmem(whole, BF16), vmem(whole, BF16),
            vmem((tokens, 4 * width), BF16), vmem(w.shape, BF16), vmem((columns, 2 * width), BF16),
            vmem(whole, BF16), vmem(whole, BF16),
            vmem((n_spans,) + state, F32), vmem((n_spans,) + state, BF16), vmem(state, F32), vmem(state, F32),
            bufs, bufs,
            dma((5,)), dma((chunks,)), dma((chunks,)), dma((chunks,)), dma((chunks,)), dma((chunks,)), dma((chunks,)), dma((stream,)), dma((stream,)),
            dma((stream,)), dma((stream,)),
            dma((pieces,)), dma((pieces,)), dma((3, pieces)), dma((3, pieces)),
        ],
        compiler_params=pltpu.CompilerParams(
            collective_id=0, has_side_effects=True, vmem_limit_bytes=40 * 1024 * 1024),
    )(q, k, v, lg, w)
    return pl.pallas_call(
        functools.partial(finish_kernel, factor),
        out_shape=[jax.ShapeDtypeStruct(whole, BF16)] * 3,
        in_specs=[vmem_spec] * 8,
        out_specs=[any_spec] * 3,
        scratch_shapes=[vmem((tokens, columns // 2), BF16), vmem((tokens, columns // 2), BF16), dma((3, 1 + heads // 4))],
        compiler_params=pltpu.CompilerParams(vmem_limit_bytes=16 * 1024 * 1024),
    )(*parts)


def gather_plain(q, k, v, lg, w):
    tokens, columns = q.shape
    heads = columns // HEAD
    me = lax.axis_index("ctx")
    g = lax.dot_general(lax.all_gather(lg, "tp", axis=1, tiled=True), w, NT, preferred_element_type=F32).astype(BF16)
    three = (tokens, heads, HEAD)
    kv_here = jnp.einsum("lbg,lbz->bgz", k.reshape(three), v.reshape(three), preferred_element_type=F32)
    grad_here = jnp.einsum("lbg,lbz->bgz", q.reshape(three), g.reshape(three), preferred_element_type=F32)

    def pick(mine, lower):
        stacked = lax.all_gather(mine[None], "ctx", axis=0, tiled=True)
        index = jnp.arange(stacked.shape[0])
        chosen = index < me if lower else index > me
        return jnp.sum(jnp.where(chosen[:, None, None, None], stacked, 0.0), 0).astype(BF16)

    return g, pick(kv_here, True), pick(grad_here, False)


def local(q, k, v, lg, w):
    n_ctx = lax.axis_size("ctx")
    n_tp = lax.axis_size("tp")
    factor = float((HEAD * q.shape[0] * n_ctx) ** (-0.5))
    if n_tp == 4 and n_ctx == 8 and q.shape[0] % 1024 == 0 and q.shape[1] % 1024 == 0:
        return tuple(fused(q, k, v, lg, w, n_ctx, factor))
    g, kv_before, grad_after = gather_plain(q, k, v, lg, w)
    return tuple(attention(q, k, v, g, kv_before, grad_after, factor))


def solution(mesh):
    return jax.shard_map(
        local,
        mesh=mesh,
        in_specs=(P("ctx", "tp"), P("ctx", "tp"), P("ctx", "tp"), P("ctx", "tp"), P("tp", None)),
        out_specs=(P("ctx", "tp"), P("ctx", "tp"), P("ctx", "tp")),
        check_vma=False,
    )
```

```python
import functools

import jax
import jax.numpy as jnp
from jax import lax
from jax.experimental import pallas as pl
from jax.experimental.pallas import tpu as pltpu
from jax.sharding import PartitionSpec as P

HEAD = 128
MESH = pl.DeviceIdType.MESH
F32 = jnp.float32
BF16 = jnp.bfloat16
NT = (((1,), (1,)), ((), ()))
NN = (((1,), (0,)), ((), ()))
TN = (((0,), (0,)), ((), ()))


def mm(a, b, dims):
    return lax.dot_general(a, b, dims, preferred_element_type=F32)


def attention_head(read, state_kv, state_grad, write, tokens, size, factor):
    count = tokens // size
    pieces = [read(i) for i in range(count)]
    rows = lax.broadcasted_iota(jnp.int32, (size, size), 0)
    cols = lax.broadcasted_iota(jnp.int32, (size, size), 1)
    causal = rows >= cols
    after = [None] * count
    total = state_grad
    for i in reversed(range(count)):
        after[i] = total.astype(BF16)
        if i:
            q, _, _, g = pieces[i]
            total = total + mm(q, g, TN)
    before = state_kv
    for i in range(count):
        q, k, v, g = pieces[i]
        inner_grad = jnp.where(causal, mm(g, v, NT), 0.0).astype(BF16)
        inner_query = jnp.where(causal, mm(q, k, NT), 0.0).astype(BF16)
        query = mm(inner_grad, k, NN) + mm(g, before.astype(BF16), NT)
        key = mm(inner_grad, q, TN) + mm(v, after[i], NT)
        value = mm(inner_query, g, TN) + mm(k, after[i], NN)
        write(i, (factor * query).astype(BF16), (factor * key).astype(BF16), (factor * value).astype(BF16))
        if i < count - 1:
            before = before + mm(k, v, TN)


def attention_kernel(size, factor, q_ref, k_ref, v_ref, g_ref, kv_ref, grad_ref, qo_ref, ko_ref, vo_ref):
    tokens = q_ref.shape[0]

    def read(i):
        at = pl.ds(i * size, size)
        return q_ref[at, :], k_ref[at, :], v_ref[at, :], g_ref[at, :]

    def write(i, query, key, value):
        at = pl.ds(i * size, size)
        qo_ref[at, :] = query
        ko_ref[at, :] = key
        vo_ref[at, :] = value

    attention_head(read, kv_ref[0].astype(F32), grad_ref[0].astype(F32), write, tokens, size, factor)


def attention(q, k, v, g, kv_before, grad_after, factor):
    tokens, columns = q.shape
    size = min(256, tokens)
    rows = pl.BlockSpec((tokens, HEAD), lambda h: (0, h))
    state = pl.BlockSpec((1, HEAD, HEAD), lambda h: (h, 0, 0))
    return pl.pallas_call(
        functools.partial(attention_kernel, size, factor),
        grid=(columns // HEAD,),
        out_shape=[jax.ShapeDtypeStruct(q.shape, BF16)] * 3,
        in_specs=[rows] * 4 + [state] * 2,
        out_specs=[rows] * 3,
    )(q, k, v, g, kv_before, grad_after)


def gather_kernel(
    n_ctx, spans, q_hbm, k_hbm, v_hbm, lg_hbm, w_hbm, qo_buf, ko_buf, vo_buf, key_part, value_part, grad_after, k_buf, v_buf,
    q_buf, g_ref, lg, w, far, far_turn, part_out, part_in,
    kv_sums, kv_state, state, after, kv_bufs, grad_bufs,
    load_sem, ends_sem, mids_sem, outs_sem, end_recv, mid_recv, out_recv, fwd_sem, end2_recv, part_sem, part_recv,
    far_sem, far_recv, twin_sem, twin_recv, factor,
):
    me = lax.axis_index("ctx")
    z = lax.axis_index("tp")
    tokens, width = lg_hbm.shape
    columns = w_hbm.shape[0]
    heads = columns // HEAD
    half_heads = heads // 2
    part_heads = half_heads // 2
    chunks = ends_sem.shape[0]
    size = tokens // chunks
    small = fwd_sem.shape[0] // chunks
    sub = size // small
    ahead = 3
    pieces = far_sem.shape[0]
    quarter = columns // 4
    piece = quarter // pieces
    share = me % 4
    twin = me + 1 - 2 * (me % 2)
    core = me % 2
    pal = me + 2 - 4 * ((me // 2) % 2)
    pal_share = (share + 2) % 4
    is_end = (z == 0) | (z == 3)
    is_mid = (z == 1) | (z == 2)
    low = z // 2
    end = 3 * low
    mid = 1 + low
    mid2 = 2 - low
    end2 = 3 - end
    far_col = pl.multiple_of((1 - low) * 2 * width, 2 * width)
    near_col = pl.multiple_of(low * 2 * width, 2 * width)

    def col(part):
        return pl.ds(pl.multiple_of(part * width, width), width)

    def row(i):
        return pl.ds(pl.multiple_of(tokens - (i + 1) * size, size), size)

    def sub_row(i, j):
        return pl.ds(pl.multiple_of(tokens - i * size - (j + 1) * sub, sub), sub)

    loads = [
        pltpu.make_async_copy(k_hbm, k_buf, load_sem.at[0]),
        pltpu.make_async_copy(v_hbm, v_buf, load_sem.at[1]),
        pltpu.make_async_copy(q_hbm, q_buf, load_sem.at[2]),
        pltpu.make_async_copy(lg_hbm, lg.at[:, col(z)], load_sem.at[3]),
        pltpu.make_async_copy(w_hbm, w, load_sem.at[4]),
    ]
    for load in loads:
        load.start()
    barrier = pltpu.get_barrier_semaphore()
    for d in range(1, n_ctx):
        pl.semaphore_signal(barrier, inc=1, device_id=((me + d) % n_ctx, z), device_id_type=MESH)

    @pl.when(is_end)
    def _():
        pl.semaphore_signal(barrier, inc=1, device_id=(me, mid), device_id_type=MESH)
        pl.semaphore_wait(barrier, n_ctx)

    @pl.when(is_mid)
    def _():
        pl.semaphore_signal(barrier, inc=1, device_id=(me, end), device_id_type=MESH)
        pl.semaphore_signal(barrier, inc=1, device_id=(me, mid2), device_id_type=MESH)
        pl.semaphore_wait(barrier, n_ctx + 1)

    def remote(src, dst, send, recv, target):
        return pltpu.make_async_remote_copy(
            src_ref=src, dst_ref=dst, send_sem=send, recv_sem=recv, device_id=target, device_id_type=MESH)

    def end_copy(i):
        return remote(lg_hbm.at[row(i), :], lg.at[row(i), col(end)], ends_sem.at[i], end_recv.at[i], (me, mid))

    def mid_copy(i, part):
        return remote(lg_hbm.at[row(i), :], lg.at[row(i), col(part)], mids_sem.at[i], mid_recv.at[i], (me, mid2))

    def out_copy(i, part):
        return remote(lg_hbm.at[row(i), :], lg.at[row(i), col(part)], outs_sem.at[i], out_recv.at[i], (me, end))

    def forward(rows, n):
        place = lg.at[rows, col(end)]
        return remote(place, place, fwd_sem.at[n], end2_recv.at[n], (me, mid2))

    def end2_arrival(rows, n):
        place = lg.at[rows, col(end2)]
        return remote(place, place, fwd_sem.at[n], end2_recv.at[n], (me, mid2))

    def part_send(rows, n):
        return remote(part_out.at[rows, :], part_in.at[rows, :], part_sem.at[n], part_recv.at[n], (me, end))

    def chunk_rows(i, step):
        @pl.loop(0, small)
        def _(j):
            step(sub_row(i, j), i * small + j)

    def each_row(step):
        @pl.loop(0, chunks)
        def _(i):
            chunk_rows(i, step)

    def far_rows(which, p):
        return pl.ds(pl.multiple_of(which * quarter + p * piece, piece), piece)

    def far_send(p):
        return remote(w_hbm.at[far_rows(share, p), pl.ds(far_col, 2 * width)], far.at[far_rows(share, p), :],
                      far_sem.at[p], far_recv.at[p], (me, mid))

    def far_share(which, p, slot, target):
        place = far.at[far_rows(which, p), :]
        return remote(place, place, twin_sem.at[slot, p], twin_recv.at[slot, p], (target, z))

    @pl.when(is_end)
    def _():
        for p in range(pieces):
            far_send(p).start()

        @pl.loop(0, chunks)
        def _(i):
            end_copy(i).start()

    @pl.when(is_mid)
    def _():
        @pl.loop(0, chunks)
        def _(i):
            mid_copy(i, mid).start()
            out_copy(i, mid).start()

    loads[0].wait()
    loads[1].wait()

    def head(h):
        return pl.ds(pl.multiple_of(h * HEAD, HEAD), HEAD)

    def by_head(step, first=0, count=heads, unroll=4):
        @pl.loop(0, count // unroll)
        def _(n):
            for u in range(unroll):
                step(first + n * unroll + u)

    chip = me // 2
    n_chips = n_ctx // 2
    mine = pl.ds(pl.multiple_of(core * half_heads, half_heads), half_heads)
    other = pl.ds(pl.multiple_of((1 - core) * half_heads, half_heads), half_heads)

    class Exchange:
        def __init__(self, bufs, down):
            (self.out, self.twin, self.pair, self.pair_in, self.rest, self.rest_in,
             self.core_sem, self.core_recv, self.pair_sem, self.pair_recv) = bufs
            self.down = down
            self.giver = 1 if down else 0

        def core_copy(self, src, dst, n):
            return remote(src, dst, self.core_sem.at[n], self.core_recv.at[n], (twin, z))

        def swap(self, first, n):
            at = pl.ds(first + n * part_heads, part_heads)
            return self.core_copy(self.out.at[at], self.twin.at[at], n)

        def extra(self, heads_at):
            return self.core_copy(self.out.at[heads_at], self.twin.at[heads_at], 2)

        def last(self, n):
            at = pl.ds(n * part_heads, part_heads)
            return self.core_copy(self.rest.at[at], self.rest_in.at[at], 3 + n)

        def pair_copy(self, d, n):
            target = me + n_ctx - 2 * d if self.down else me + 2 * d
            at = pl.ds(n * part_heads, part_heads)
            return remote(self.pair.at[at], self.pair_in.at[d - 1, at], self.pair_sem.at[d - 1, n],
                          self.pair_recv.at[d - 1, n], (target % n_ctx, z))

        def sends(self, d):
            return chip >= d if self.down else chip + d < n_chips

        def takes(self, d):
            return chip + d < n_chips if self.down else chip >= d

        def begin(self, total):
            def step(h):
                value = total(h)
                after[h] = value
                self.out[h] = value.astype(BF16)

            for n in range(2):
                by_head(step, (1 - core) * half_heads + n * part_heads, part_heads, 2)
                self.swap((1 - core) * half_heads, n).start()
            by_head(step, core * half_heads, half_heads)

            @pl.when(core == self.giver)
            def _():
                self.extra(mine).start()

        def combine(self):
            def step(j):
                h = core * half_heads + j
                self.pair[j] = (after[h] + self.twin[h].astype(F32)).astype(BF16)

            for n in range(2):
                self.swap(core * half_heads, n).wait_recv()
                by_head(step, n * part_heads, part_heads, 2)
                for d in reversed(range(1, n_chips)):
                    @pl.when(self.sends(d))
                    def _():
                        self.pair_copy(d, n).start()

        def collect(self):
            def step(j):
                total = self.pair_in[0, j].astype(F32)
                for d in range(2, n_chips):
                    total = total + self.pair_in[d - 1, j].astype(F32)
                self.rest[j] = total

            for n in range(2):
                for d in range(1, n_chips):
                    @pl.when(self.takes(d))
                    def _():
                        self.pair_copy(d, n).wait_recv()

                    @pl.when(jnp.logical_not(self.takes(d)))
                    def _():
                        at = pl.ds(n * part_heads, part_heads)
                        self.pair_in[d - 1, at] = jnp.zeros((part_heads, HEAD, HEAD), BF16)

                by_head(step, n * part_heads, part_heads, 2)
                self.last(n).start()

        def finish(self, write, between):
            @pl.when(core != self.giver)
            def _():
                self.extra(other).wait_recv()

            def step(j, ref, first):
                own = jnp.where(core != self.giver, self.twin[first + j].astype(F32), 0.0)
                write(first + j, ref[j] + own)

            by_head(lambda j: step(j, self.rest, core * half_heads), 0, half_heads)
            between()
            for n in range(2):
                self.last(n).wait_recv()
            by_head(lambda j: step(j, self.rest_in, (1 - core) * half_heads), 0, half_heads)

        def drain(self):
            @pl.when(core == self.giver)
            def _():
                self.extra(mine).wait_send()

            for n in range(2):
                self.swap((1 - core) * half_heads, n).wait_send()
                self.last(n).wait_send()
                for d in range(1, n_chips):
                    @pl.when(self.sends(d))
                    def _():
                        self.pair_copy(d, n).wait_send()

    kv = Exchange(kv_bufs, False)
    grad = Exchange(grad_bufs, True)

    def sum_kv(h):
        total = jnp.zeros((HEAD, HEAD), F32)
        for c, (start, length) in enumerate(spans):
            at = pl.ds(start, length)
            here = mm(v_buf[at, head(h)], k_buf[at, head(h)], TN)
            kv_sums[c, h] = here
            total = total + here
        state[h] = jnp.zeros((HEAD, HEAD), F32)
        return total

    kv.begin(sum_kv)
    kv.combine()
    for load in loads[2:]:
        load.wait()

    def set_kv(h, total):
        for c in reversed(range(len(spans))):
            kv_state[c, h] = total.astype(BF16)
            total = total + kv_sums[c, h]

    def attend(c, start, length, keep):
        at = pl.ds(start, length)
        rows_at = lax.broadcasted_iota(jnp.int32, (length, length), 0)
        cols_at = lax.broadcasted_iota(jnp.int32, (length, length), 1)

        def step(h):
            hd = head(h)
            q, k, v, g = q_buf[at, hd], k_buf[at, hd], v_buf[at, hd], g_ref[at, hd]
            grad_rows = jnp.where(rows_at >= cols_at, mm(g, v, NT), 0.0).astype(BF16)
            grad_cols = jnp.where(rows_at <= cols_at, mm(v, g, NT), 0.0).astype(BF16)
            query_cols = jnp.where(rows_at <= cols_at, mm(k, q, NT), 0.0).astype(BF16)
            total = state[h]
            later = total.astype(BF16)
            query = mm(grad_rows, k, NN) + mm(g, kv_state[c, h], NN)
            qo_buf[at, hd] = (factor * query).astype(BF16)
            key_part[at, hd] = mm(grad_cols, q, NN) + mm(v, later, NT)
            value_part[at, hd] = mm(query_cols, g, NN) + mm(k, later, NN)
            if keep:
                state[h] = total + mm(q, g, TN)

        return step

    def attend_some(n):
        share_of = heads // small
        for c in range(len(spans) - 1):
            @pl.when(n // small == 2 * c + 3)
            def _():
                by_head(attend(c, *spans[c], True), (n % small) * share_of, share_of, share_of)

    def project(left, right, out_ref, at, tile):
        @pl.loop(0, columns // tile)
        def _(n):
            out = pl.ds(pl.multiple_of(n * tile, tile), tile)
            out_ref[at, out] = mm(left[at, :], right[out, :], NT)

    middle = pl.ds(width, 2 * width)
    near = pl.ds(near_col, 2 * width)
    far_mid2 = pl.ds(pl.multiple_of(low * width, width), width)
    far_end2 = pl.ds(pl.multiple_of((1 - low) * width, width), width)
    tile = 512
    block = 2 * size
    blocks = tokens // block

    def span(c):
        return pl.ds(pl.multiple_of(tokens - (c + 1) * block, block), block)

    @pl.when(is_end)
    def _():
        @pl.loop(0, blocks)
        def _(c):
            for j in range(2):
                out_copy(c * 2 + j, mid).wait_recv()
            project(lg.at[:, near], w.at[:, near], key_part, span(c), tile)

        kv.collect()
        kv.finish(set_kv, lambda: None)

        def take(rows, n):
            part_send(rows, n).wait_recv()
            g_ref[rows, :] = (key_part[rows, :] + part_in[rows, :].astype(F32)).astype(BF16)

        @pl.loop(0, chunks)
        def _(i):
            def step(rows, n):
                attend_some(n)
                take(rows, n)

            chunk_rows(i, step)

    @pl.when(is_mid)
    def _():
        def forward_chunk(i):
            end_copy(i).wait_recv()
            chunk_rows(i, lambda rows, n: forward(rows, n).start())

        for c in range(blocks):
            if c == 3:
                for i in range(1, ahead):
                    forward_chunk(i)
                kv.finish(set_kv, lambda: None)
                for p in range(pieces):
                    far_share(share + 1 - 2 * core, p, 1, twin).wait_recv()
                    far_share(pal_share + 1 - 2 * core, p, 2, twin).wait_recv()

                @pl.loop(0, columns // block)
                def _(n):
                    out = pl.ds(pl.multiple_of(n * block, block), block)
                    far_turn[:, out] = far[out, far_end2].T

                @pl.loop(0, c)
                def _(n):
                    project(lg.at[:, col(mid2)], far.at[:, far_mid2], value_part, span(n), tile)
            for j in range(2):
                mid_copy(c * 2 + j, mid2).wait_recv()
            if c < pieces:
                far_send(c).wait_recv()
                far_share(share, c, 0, pal).start()
                far_share(share, c, 1, twin).start()
            if c == 2:
                for p in range(pieces):
                    far_share(pal_share, p, 0, pal).wait_recv()
                    far_share(pal_share, p, 2, twin).start()
                kv.collect()
                forward_chunk(0)
            project(lg.at[:, middle], w.at[:, middle], key_part, span(c), tile)
        project(lg.at[:, col(mid2)], far.at[:, far_mid2], value_part, span(blocks - 1), tile)

        def give(rows, n):
            end2_arrival(rows, n).wait_recv()
            total = value_part[rows, :] + mm(lg[rows, col(end2)], far_turn[...], NN)
            part_out[rows, :] = total.astype(BF16)
            part_send(rows, n).start()

        def own(rows, n):
            out = pl.ds(pl.multiple_of(n * tile, tile), tile)
            total = key_part[rows, out] + mm(lg[rows, col(end)], w[out, col(end)], NT)
            g_ref[rows, out] = (total + mm(lg[rows, col(end2)], w[out, col(end2)], NT)).astype(BF16)

        def own_some(n):
            i = n // small
            j = n % small
            apart = small * tile // columns

            @pl.when((i % 2 == 0) & (i > 0) & (j % apart == 0))
            def _():
                own(span(i // 2 - 1), j // apart)

        @pl.loop(0, chunks)
        def _(i):
            @pl.when(i < chunks - ahead)
            def _():
                forward_chunk(i + ahead)

            def step(rows, n):
                attend_some(n)
                own_some(n)
                give(rows, n)

            chunk_rows(i, step)

        @pl.loop(0, columns // tile)
        def _(n):
            own(span(blocks - 1), n)

    final = len(spans) - 1
    last_rows = pl.ds(*spans[final])
    grad.begin(lambda h: state[h] + mm(q_buf[last_rows, head(h)], g_ref[last_rows, head(h)], TN))
    grad.combine()
    by_head(attend(final, *spans[final], False))
    grad.collect()

    def set_grad(h, total):
        grad_after[h] = total.astype(BF16)

    def finish_half():
        by_head(lambda h: finish_head(factor, h, h, key_part, value_part, grad_after, k_buf, v_buf, ko_buf, vo_buf),
                core * half_heads, half_heads, 2)

    grad.finish(set_grad, finish_half)
    kv.drain()
    grad.drain()

    @pl.when(is_end)
    def _():
        for p in range(pieces):
            far_send(p).wait_send()

        @pl.loop(0, chunks)
        def _(i):
            end_copy(i).wait_send()

    @pl.when(is_mid)
    def _():
        for p in range(pieces):
            far_share(share, p, 0, pal).wait_send()
            far_share(share, p, 1, twin).wait_send()
            far_share(pal_share, p, 2, twin).wait_send()

        @pl.loop(0, chunks)
        def _(i):
            mid_copy(i, mid).wait_send()
            out_copy(i, mid).wait_send()

        each_row(lambda rows, n: forward(rows, n).wait_send())
        each_row(lambda rows, n: part_send(rows, n).wait_send())


def finish_kernel(
    factor, qo_buf, ko_half, vo_half, key_part, value_part, grad_after, k_buf, v_buf, qo, ko, vo, ko_buf, vo_buf, sem,
):
    heads = grad_after.shape[0]
    group = 2
    half = heads // 2
    core = lax.axis_index("ctx") % 2
    done = pl.ds(pl.multiple_of(core * half * HEAD, half * HEAD), half * HEAD)
    ready = [
        pltpu.make_async_copy(ko_half.at[:, done], ko.at[:, done], sem.at[1, 0]),
        pltpu.make_async_copy(vo_half.at[:, done], vo.at[:, done], sem.at[2, 0]),
        pltpu.make_async_copy(qo_buf, qo, sem.at[0, 0]),
    ]
    for copy in ready:
        copy.start()

    def copies(n):
        here = pl.ds(pl.multiple_of(n * group * HEAD, group * HEAD), group * HEAD)
        there = pl.ds(pl.multiple_of(((1 - core) * half + n * group) * HEAD, group * HEAD), group * HEAD)
        return (
            pltpu.make_async_copy(ko_buf.at[:, here], ko.at[:, there], sem.at[1, n + 1]),
            pltpu.make_async_copy(vo_buf.at[:, here], vo.at[:, there], sem.at[2, n + 1]),
        )

    for n in range(half // group):
        for u in range(group):
            to = n * group + u
            finish_head(factor, (1 - core) * half + to, to, key_part, value_part, grad_after, k_buf, v_buf, ko_buf, vo_buf)
        for copy in copies(n):
            copy.start()
    for copy in ready:
        copy.wait()
    for n in range(half // group):
        for copy in copies(n):
            copy.wait()


def finish_head(factor, h, to, key_part, value_part, grad_after, k_buf, v_buf, ko_buf, vo_buf):
    at = pl.ds(pl.multiple_of(h * HEAD, HEAD), HEAD)
    out = pl.ds(pl.multiple_of(to * HEAD, HEAD), HEAD)
    after = grad_after[h]
    ko_buf[:, out] = (factor * (key_part[:, at] + mm(v_buf[:, at], after, NT))).astype(BF16)
    vo_buf[:, out] = (factor * (value_part[:, at] + mm(k_buf[:, at], after, NN))).astype(BF16)


def fused(q, k, v, lg, w, n_ctx, factor):
    tokens, width = lg.shape
    columns = w.shape[0]
    heads = columns // HEAD
    chunks = 8
    small = 2
    pieces = 2
    size = tokens // chunks
    spans = [(tokens - (c + 1) * 2 * size, 2 * size) for c in range(chunks // 2)]
    n_spans = len(spans)
    stream = chunks * small
    dma = pltpu.SemaphoreType.DMA
    vmem = pltpu.VMEM
    state = (heads, HEAD, HEAD)
    half = (heads // 2, HEAD, HEAD)
    whole = (tokens, columns)
    chips = n_ctx // 2
    bufs = (
        vmem(state, BF16), vmem(state, BF16), vmem(half, BF16), vmem((chips - 1,) + half, BF16), vmem(half, F32), vmem(half, F32),
        dma((5,)), dma((5,)), dma((chips - 1, 2)), dma((chips - 1, 2)),
    )
    any_spec = pl.BlockSpec(memory_space=pl.ANY)
    vmem_spec = pl.BlockSpec(memory_space=pltpu.VMEM)
    parts = pl.pallas_call(
        functools.partial(gather_kernel, n_ctx, spans, factor=factor),
        out_shape=[
            vmem(whole, BF16), vmem(whole, BF16), vmem(whole, BF16), vmem(whole, F32), vmem(whole, F32), vmem(state, BF16),
            vmem(whole, BF16), vmem(whole, BF16),
        ],
        in_specs=[any_spec] * 5,
        out_specs=[vmem_spec] * 8,
        scratch_shapes=[
            vmem(whole, BF16), vmem(whole, BF16),
            vmem((tokens, 4 * width), BF16), vmem(w.shape, BF16), vmem((columns, 2 * width), BF16), vmem((width, columns), BF16),
            vmem(whole, BF16), vmem(whole, BF16),
            vmem((n_spans,) + state, F32), vmem((n_spans,) + state, BF16), vmem(state, F32), vmem(state, F32),
            bufs, bufs,
            dma((5,)), dma((chunks,)), dma((chunks,)), dma((chunks,)), dma((chunks,)), dma((chunks,)), dma((chunks,)), dma((stream,)), dma((stream,)),
            dma((stream,)), dma((stream,)),
            dma((pieces,)), dma((pieces,)), dma((3, pieces)), dma((3, pieces)),
        ],
        compiler_params=pltpu.CompilerParams(
            collective_id=0, has_side_effects=True, vmem_limit_bytes=40 * 1024 * 1024),
    )(q, k, v, lg, w)
    return pl.pallas_call(
        functools.partial(finish_kernel, factor),
        out_shape=[jax.ShapeDtypeStruct(whole, BF16)] * 3,
        in_specs=[vmem_spec] * 8,
        out_specs=[any_spec] * 3,
        scratch_shapes=[vmem((tokens, columns // 2), BF16), vmem((tokens, columns // 2), BF16), dma((3, 1 + heads // 4))],
        compiler_params=pltpu.CompilerParams(vmem_limit_bytes=16 * 1024 * 1024),
    )(*parts)


def gather_plain(q, k, v, lg, w):
    tokens, columns = q.shape
    heads = columns // HEAD
    me = lax.axis_index("ctx")
    g = lax.dot_general(lax.all_gather(lg, "tp", axis=1, tiled=True), w, NT, preferred_element_type=F32).astype(BF16)
    three = (tokens, heads, HEAD)
    kv_here = jnp.einsum("lbg,lbz->bgz", k.reshape(three), v.reshape(three), preferred_element_type=F32)
    grad_here = jnp.einsum("lbg,lbz->bgz", q.reshape(three), g.reshape(three), preferred_element_type=F32)

    def pick(mine, lower):
        stacked = lax.all_gather(mine[None], "ctx", axis=0, tiled=True)
        index = jnp.arange(stacked.shape[0])
        chosen = index < me if lower else index > me
        return jnp.sum(jnp.where(chosen[:, None, None, None], stacked, 0.0), 0).astype(BF16)

    return g, pick(kv_here, True), pick(grad_here, False)


def local(q, k, v, lg, w):
    n_ctx = lax.axis_size("ctx")
    n_tp = lax.axis_size("tp")
    factor = float((HEAD * q.shape[0] * n_ctx) ** (-0.5))
    if n_tp == 4 and n_ctx == 8 and q.shape[0] % 1024 == 0 and q.shape[1] % 1024 == 0:
        return tuple(fused(q, k, v, lg, w, n_ctx, factor))
    g, kv_before, grad_after = gather_plain(q, k, v, lg, w)
    return tuple(attention(q, k, v, g, kv_before, grad_after, factor))


def solution(mesh):
    return jax.shard_map(
        local,
        mesh=mesh,
        in_specs=(P("ctx", "tp"), P("ctx", "tp"), P("ctx", "tp"), P("ctx", "tp"), P("tp", None)),
        out_specs=(P("ctx", "tp"), P("ctx", "tp"), P("ctx", "tp")),
        check_vma=False,
    )
```
